32 devices in a mesh: seq: 8 (over z, y), head: 4 (over x, core).
Axes of the slice: x: 2, y: 2, z: 4, core: 2. Of those that a mesh axis runs over, the one named last changes fastest.
Arguments:
- queries: bfloat16 [1024, 4096], P(('seq', 'head')), may hold values from -6 to 6
- keys: bfloat16 [1024, 4096], P(('seq', 'head')), may hold values from -0.5 to 0.5
- values: bfloat16 [1024, 4096], P(('seq', 'head')), may hold values from -6 to 6
- log_decay: float32 [1024, 32], P('seq', 'head'), may hold values from -2 to 0, as said below
- out_grad: bfloat16 [1024, 4096], P('seq', 'head'), may hold values from -6 to 6
Outputs:
- attn_out: bfloat16 [1024, 4096], P('seq', 'head')
- query_grad: bfloat16 [1024, 4096], P('seq', 'head')
- key_grad: bfloat16 [1024, 4096], P('seq', 'head')
- value_grad: bfloat16 [1024, 4096], P('seq', 'head')
The draws below stay inside these ranges and needn't reach their ends.
Inputs may be any that keep to these rules, and one draw needn't show every extreme that they name: `log_decay`: never positive.
All inputs are finite; a program needn't handle non-finite values.
Results may differ from the reference program's by a relative error of at most 0.0056.
Values may be sent and summed in bfloat16 or wider, within the bound.
No kernel may reach another device: no remote copies, remote signals or barrier semaphores. Data moves between devices by JAX's collectives and lax.ppermute only.
A program may use at most 64 MiB of HBM per device.

```python
import jax
import jax.numpy as jnp
from jax import lax

HEAD_GROUP = 32
DK = 128
TOK_DEV = 32
BLOCK = 128
SEQUENCE_TOKENS = 1024


def draw_log_decay(key, part):
    key_sequence = jax.random.split(key, 7)
    fast_share = 0.5
    fast_heads = jax.random.uniform(key_sequence[0], (HEAD_GROUP,), jnp.float32) < fast_share
    fast_rate = jnp.exp(jax.random.uniform(key_sequence[1], (HEAD_GROUP,), jnp.float32, jnp.log(1.0 / 50.0), jnp.log(1.0 / 30.0)))
    slow_rate = jax.random.uniform(key_sequence[2], (HEAD_GROUP,), jnp.float32, 0.2, 0.7) / SEQUENCE_TOKENS
    baseline_rate = jnp.where(fast_heads, fast_rate, slow_rate)
    block_multiplier = jnp.exp(jax.random.uniform(key_sequence[3], (SEQUENCE_TOKENS // TOK_DEV, HEAD_GROUP), jnp.float32, -0.5, 0.5))
    block_multiplier = jnp.repeat(block_multiplier, TOK_DEV, axis=0)
    token_multiplier = jax.random.uniform(key_sequence[4], (SEQUENCE_TOKENS, HEAD_GROUP), jnp.float32, 0.5, 1.5)
    spike_position = jax.random.randint(key_sequence[5], (3, HEAD_GROUP), 0, SEQUENCE_TOKENS)
    spike_loss = jax.random.uniform(key_sequence[6], (3, HEAD_GROUP), jnp.float32, 0.2, 0.4)
    spike_hits = jnp.arange(SEQUENCE_TOKENS, dtype=jnp.int32)[:, None, None] == spike_position[None]
    spike_events = jnp.sum(jnp.where(spike_hits, jnp.log1p(-spike_loss)[None], 0.0), axis=1)
    return (-(baseline_rate[None, :] * block_multiplier * token_multiplier) + spike_events).astype(jnp.float32)


def block_levels(key, dims, pieces, least, high):
    def one(axis_at, shards_of):
        steps = jax.random.uniform(jax.random.fold_in(jax.random.fold_in(key, 6), axis_at), (shards_of,), jnp.float32, least / len(pieces), high / len(pieces))
        return jnp.repeat(jnp.exp(steps), dims[axis_at] // shards_of).reshape((-1,) + (1,) * (len(dims) - axis_at - 1))

    gain = one(*pieces[0])
    for cut in pieces[1:]:
        gain = gain * one(*cut)
    return gain


def scatter_about(stream_key, dims, deviation, bound, cuts=(), held_as=jnp.bfloat16):
    drawn = jax.random.normal(stream_key, dims, jnp.float32) * deviation
    if len(cuts) > 0:
        drawn = block_levels(stream_key, dims, cuts, -0.22, 0.18) * drawn
    return jnp.clip(drawn, min=-bound, max=bound).astype(held_as)


def setup_inputs(seed: int = 0) -> dict:
    key_of = jax.random.split(jax.random.key(seed), 6)
    return {
        "queries": scatter_about(key_of[0], (SEQUENCE_TOKENS, HEAD_GROUP * DK), 1.0, 6.0, ((0, 32),)),
        "keys": scatter_about(key_of[1], (SEQUENCE_TOKENS, HEAD_GROUP * DK), DK ** -0.5, 0.5, ((0, 32),)),
        "values": scatter_about(key_of[2], (SEQUENCE_TOKENS, HEAD_GROUP * DK), 1.0, 6.0, ((0, 32),)),
        "log_decay": draw_log_decay(jax.random.fold_in(key_of[5], 71), 0),
        "out_grad": scatter_about(key_of[4], (SEQUENCE_TOKENS, HEAD_GROUP * DK), 1.0, 6.0, ((0, 8), (1, 4))),
    }


exact_mode = lax.Precision.HIGHEST

def decay_table(running):
    block_rows = running.shape[0]
    gaps = running.T[:, :, None] - running.T[:, None, :]
    causal = lax.broadcasted_iota(jnp.int32, (block_rows, block_rows), 0) >= lax.broadcasted_iota(jnp.int32, (block_rows, block_rows), 1)
    return jnp.where(causal[None], jnp.exp(jnp.where(causal[None], gaps, 0.0)), 0.0)

def block_forward(query_block, key_block, value_block, decay_block, grad_block, state):
    running = jnp.cumsum(decay_block, axis=0)
    final = running[-1]
    table = decay_table(running)
    query_wide = query_block.astype(jnp.float32)
    key_wide = key_block.astype(jnp.float32)
    value_wide = value_block.astype(jnp.float32)
    scores = jnp.einsum('thd,shd->hts', query_wide, key_wide)
    weighted = (scores * table).astype(jnp.bfloat16)
    inner = jnp.einsum('hts,she->the', weighted.astype(jnp.float32), value_wide)
    carried = jnp.einsum('thd,hde->the', query_wide, state, precision=exact_mode) * jnp.exp(running)[:, :, None]
    mixed = inner + carried
    inverse = lax.rsqrt(lax.optimization_barrier(jnp.mean(mixed * mixed, axis=-1)) + 1e-06)
    normed = mixed * inverse[:, :, None]
    grad_wide = grad_block.astype(jnp.float32)
    out_delta = (inverse[:, :, None] * (grad_wide - normed * lax.optimization_barrier(jnp.mean(grad_wide * normed, axis=-1, keepdims=True)))).astype(jnp.bfloat16)
    tail_weight = jnp.exp(final[None, :] - running)
    own_state = jnp.einsum('thd,the->hde', key_wide * tail_weight[:, :, None], value_wide, precision=exact_mode)
    own_grad = jnp.einsum('thd,the->hde', query_wide * jnp.exp(running)[:, :, None], out_delta.astype(jnp.float32), precision=exact_mode)
    return (normed.astype(jnp.bfloat16), out_delta, own_state, own_grad, jnp.exp(final))

def block_backward(query_block, key_block, value_block, decay_block, out_delta, state, grad_state):
    running = jnp.cumsum(decay_block, axis=0)
    final = running[-1]
    table = decay_table(running)
    query_wide = query_block.astype(jnp.float32)
    key_wide = key_block.astype(jnp.float32)
    value_wide = value_block.astype(jnp.float32)
    delta_wide = out_delta.astype(jnp.float32)
    weighted = (jnp.einsum('thd,shd->hts', query_wide, key_wide) * table).astype(jnp.bfloat16).astype(jnp.float32)
    delta_weighted = (jnp.einsum('the,she->hts', delta_wide, value_wide) * table).astype(jnp.bfloat16).astype(jnp.float32)
    tail_weight = jnp.exp(final[None, :] - running)[:, :, None]
    query_grad = jnp.einsum('hts,shd->thd', delta_weighted, key_wide) + jnp.exp(running)[:, :, None] * jnp.einsum('the,hde->thd', delta_wide, state, precision=exact_mode)
    key_grad = jnp.einsum('hts,thd->shd', delta_weighted, query_wide) + tail_weight * jnp.einsum('she,hde->shd', value_wide, grad_state, precision=exact_mode)
    value_grad = jnp.einsum('hts,the->she', weighted, delta_wide) + tail_weight * jnp.einsum('shd,hde->she', key_wide, grad_state, precision=exact_mode)
    return (query_grad.astype(jnp.bfloat16), key_grad.astype(jnp.bfloat16), value_grad.astype(jnp.bfloat16))

def reference(queries, keys, values, log_decay, out_grad):
    block_count = SEQUENCE_TOKENS // BLOCK
    layout = (block_count, BLOCK, HEAD_GROUP, DK)
    query_blocks = queries.reshape(layout)
    key_blocks = keys.reshape(layout)
    value_blocks = values.reshape(layout)
    decay_blocks = log_decay.reshape(block_count, BLOCK, HEAD_GROUP)
    grad_blocks = out_grad.reshape(layout)
    empty = jnp.zeros((HEAD_GROUP, DK, DK), jnp.float32)

    def forward_step(state, item):
        normed, out_delta, own_state, own_grad, factor = block_forward(item[0], item[1], item[2], item[3], item[4], state)
        following = factor[:, None, None] * state + own_state
        return (following, (normed, out_delta, state, own_grad, factor))
    unused, saved = lax.scan(forward_step, empty, (query_blocks, key_blocks, value_blocks, decay_blocks, grad_blocks))
    outputs, deltas, states, own_grads, factors = saved

    def backward_step(carry, item):
        return (item[1][:, None, None] * carry + item[0], carry)
    unused_too, grad_states = lax.scan(backward_step, empty, (own_grads, factors), reverse=True)

    def gradients(item):
        return block_backward(item[0], item[1], item[2], item[3], item[4], item[5], item[6])
    query_grad, key_grad, value_grad = lax.map(gradients, (query_blocks, key_blocks, value_blocks, decay_blocks, deltas, states, grad_states))
    flat = (SEQUENCE_TOKENS, HEAD_GROUP * DK)
    return (outputs.reshape(flat), query_grad.reshape(flat), key_grad.reshape(flat), value_grad.reshape(flat))
```

```python
import functools

import jax
import jax.numpy as jnp
from jax import lax
from jax.experimental import pallas as pl
from jax.experimental.pallas import tpu as pltpu
from jax.sharding import PartitionSpec as P

DK = 128
F32 = jnp.float32
BF16 = jnp.bfloat16
AXES = ("seq", "head")


def power_of_two(n):
    return n & (n - 1) == 0


def mm(a, b, ca, cb, precision=None):
    return lax.dot_general(
        a, b, (((ca,), (cb,)), ((), ())), precision=precision, preferred_element_type=F32
    )


class Plan:
    def __init__(self, ns, nh, tok, block, heads):
        self.ns, self.nh, self.tok, self.block, self.heads = ns, nh, tok, block, heads
        self.g = 2 if ns % 2 == 0 and heads % 2 == 0 else 1
        self.n = self.g * nh
        self.hl = heads // self.g
        self.w = self.hl * DK
        self.tb = self.g * block
        self.nz = ns // self.g
        self.rows = max(8, self.hl)

    def partner(self, m, p):
        if power_of_two(self.n):
            return m ^ p
        return lax.rem(m + p, self.n) if not isinstance(m, int) else (m + p) % self.n

    def sender(self, m, p):
        if power_of_two(self.n):
            return m ^ p
        return lax.rem(m + self.n - p, self.n)

    def member_pairs(self, p):
        return [
            (b * self.n + m, b * self.n + self.partner(m, p))
            for b in range(self.nz)
            for m in range(self.n)
        ]

    def mate_pairs(self):
        return [
            ((s * self.nh + h), ((s ^ 1) * self.nh + h))
            for s in range(self.ns)
            for h in range(self.nh)
        ]

    def scan_pairs(self, flip):
        return [(d, ((d // self.n) ^ flip) * self.n + d % self.n) for d in range(self.nz * self.n)]

    def shift_pairs(self, by):
        total = self.nz * self.n
        return [(d, d + by * self.n) for d in range(total) if 0 <= d + by * self.n < total]


def vmem(n):
    return [pl.BlockSpec(memory_space=pltpu.VMEM)] * n


def call(kernel, outs, args, name, flops=0, scratch=()):
    size = sum(a.size * a.dtype.itemsize for a in args) + sum(
        o.size * o.dtype.itemsize for o in outs
    )
    return pl.pallas_call(
        kernel,
        out_shape=tuple(outs),
        in_specs=vmem(len(args)),
        out_specs=tuple(vmem(len(outs))),
        scratch_shapes=list(scratch),
        name=name,
        compiler_params=pltpu.CompilerParams(vmem_limit_bytes=24 * 1024 * 1024),
        cost_estimate=pl.CostEstimate(flops=flops, bytes_accessed=size, transcendentals=0),
    )(*args)


def struct(shape, dtype):
    return jax.ShapeDtypeStruct(shape, dtype)


def where_am_i(plan):
    s, h = lax.axis_index("seq"), lax.axis_index("head")
    y = lax.rem(s, plan.g)
    return y, y * plan.nh + h


def pack_kernel(plan, q_ref, k_ref, v_ref, ld_ref, *outs):
    y, m = where_am_i(plan)
    for p in range(plan.n):
        to = plan.partner(m, p)
        off = lax.rem(to, plan.nh) * (plan.heads * DK) + (to // plan.nh) * plan.w
        cols = pl.ds(pl.multiple_of(off, plan.w), plan.w)
        for i, ref in enumerate((q_ref, k_ref, v_ref)):
            outs[p][i * plan.tok : (i + 1) * plan.tok, :] = ref[:, cols]
    outs[plan.n][...] = jnp.transpose(ld_ref[...])


def split_kernel(plan, g_ref, own_ref, other_ref):
    y, m = where_am_i(plan)
    own_ref[...] = g_ref[:, pl.ds(pl.multiple_of(y * plan.w, plan.w), plan.w)]
    other_ref[...] = g_ref[:, pl.ds(pl.multiple_of((plan.g - 1 - y) * plan.w, plan.w), plan.w)]


def state_kernel(plan, *refs):
    n, tok, tb, hl = plan.n, plan.tok, plan.tb, plan.hl
    parts, (lo_ref, lp_ref) = refs[:n], refs[n : n + 2]
    q_ref, k_ref, v_ref, row_ref, col_ref, t_ref, tb_ref, f_ref = refs[n + 2 :]
    y, m = where_am_i(plan)
    for p in range(n):
        frm = plan.sender(m, p)
        at = (frm // plan.nh) * plan.block + lax.rem(frm, plan.nh) * tok
        rows = pl.ds(pl.multiple_of(at, tok), tok)
        for i, ref in enumerate((q_ref, k_ref, v_ref)):
            ref[rows, :] = parts[p][i * tok : (i + 1) * tok, :]
    pieces = []
    for i in range(plan.g):
        whole = jnp.where(y == i, lo_ref[...], lp_ref[...]) if plan.g > 1 else lo_ref[...]
        mine = whole[0:hl, :]
        for j in range(1, plan.g):
            mine = jnp.where(y == j, whole[j * hl : (j + 1) * hl, :], mine)
        pieces.append(mine)
    ld = jnp.concatenate(pieces, axis=1)
    if hl < plan.rows:
        ld = jnp.concatenate([ld, jnp.zeros((plan.rows - hl, tb), F32)], axis=0)
    upper = (
        lax.broadcasted_iota(jnp.int32, (tb, tb), 0) <= lax.broadcasted_iota(jnp.int32, (tb, tb), 1)
    ).astype(F32)
    row = mm(ld, upper, 1, 0, lax.Precision.HIGHEST)
    row_ref[...] = row
    tall = jnp.concatenate([row, jnp.zeros((128 - plan.rows, tb), F32)], axis=0)
    col = jnp.transpose(tall)
    col_ref[...] = col
    final = row[:, tb - 1 : tb]
    f_ref[...] = jnp.broadcast_to(jnp.exp(final), (plan.rows, 128))
    for h in range(hl):
        cols = slice(h * DK, (h + 1) * DK)
        tail = jnp.exp(col[tb - 1 : tb, h : h + 1] - col[:, h : h + 1])
        scaled = (k_ref[:, cols].astype(F32) * tail).astype(BF16)
        own = mm(scaled, v_ref[:, cols], 0, 0)
        t_ref[cols, :] = own
        tb_ref[cols, :] = own.astype(BF16)


def decay_of(plan, row_ref, col_ref, h):
    tb = plan.tb
    gap = col_ref[:, h : h + 1] - row_ref[h : h + 1, :]
    causal = lax.broadcasted_iota(jnp.int32, (tb, tb), 0) >= lax.broadcasted_iota(
        jnp.int32, (tb, tb), 1
    )
    return jnp.where(causal, jnp.exp(jnp.where(causal, gap, 0.0)), 0.0)


def inner_kernel(plan, q_ref, k_ref, v_ref, row_ref, col_ref, w_ref, inner_ref):
    for h in range(plan.hl):
        cols = slice(h * DK, (h + 1) * DK)
        scores = mm(q_ref[:, cols], k_ref[:, cols], 1, 1)
        weighted = (scores * decay_of(plan, row_ref, col_ref, h)).astype(BF16)
        w_ref[h] = weighted
        inner_ref[:, cols] = mm(weighted, v_ref[:, cols], 1, 0)


def mix_kernel(
    plan, q_ref, inner_ref, s_ref, own_ref, other_ref, col_ref, out_ref, od_ref, g_ref, gb_ref, gs
):
    y, m = where_am_i(plan)
    blk = plan.block
    gs[pl.ds(pl.multiple_of(y * blk, blk), blk), :] = own_ref[...]
    if plan.g > 1:
        gs[pl.ds(pl.multiple_of((1 - y) * blk, blk), blk), :] = other_ref[...]
    for h in range(plan.hl):
        cols = slice(h * DK, (h + 1) * DK)
        q = q_ref[:, cols]
        rising = jnp.exp(col_ref[:, h : h + 1])
        mixed = inner_ref[:, cols] + rising * mm(q, s_ref[cols, :].astype(BF16), 1, 0)
        inverse = lax.rsqrt(jnp.mean(mixed * mixed, axis=-1, keepdims=True) + 1e-06)
        normed = mixed * inverse
        grad = gs[:, cols].astype(F32)
        along = jnp.mean(grad * normed, axis=-1, keepdims=True)
        od = (inverse * (grad - normed * along)).astype(BF16)
        out_ref[:, cols] = normed.astype(BF16)
        od_ref[:, cols] = od
        own = mm((q.astype(F32) * rising).astype(BF16), od, 0, 0)
        g_ref[cols, :] = own
        gb_ref[cols, :] = own.astype(BF16)


def back_kernel(
    plan, q_ref, k_ref, v_ref, row_ref, col_ref, w_ref, od_ref, s_ref, qg_ref, kp_ref, vp_ref
):
    for h in range(plan.hl):
        cols = slice(h * DK, (h + 1) * DK)
        od = od_ref[:, cols]
        dscores = mm(od, v_ref[:, cols], 1, 1)
        dw = (dscores * decay_of(plan, row_ref, col_ref, h)).astype(BF16)
        rising = jnp.exp(col_ref[:, h : h + 1])
        qg = mm(dw, k_ref[:, cols], 1, 0) + rising * mm(od, s_ref[cols, :].astype(BF16), 1, 1)
        qg_ref[:, cols] = qg.astype(BF16)
        kp_ref[:, cols] = mm(dw, q_ref[:, cols], 0, 0)
        vp_ref[:, cols] = mm(w_ref[h], od, 0, 0)


def last_kernel(plan, k_ref, v_ref, col_ref, kp_ref, vp_ref, r_ref, kg_ref, vg_ref):
    tb = plan.tb
    for h in range(plan.hl):
        cols = slice(h * DK, (h + 1) * DK)
        r = r_ref[cols, :].astype(BF16)
        tail = jnp.exp(col_ref[tb - 1 : tb, h : h + 1] - col_ref[:, h : h + 1])
        kg_ref[:, cols] = (kp_ref[:, cols] + tail * mm(v_ref[:, cols], r, 1, 1)).astype(BF16)
        vg_ref[:, cols] = (vp_ref[:, cols] + tail * mm(k_ref[:, cols], r, 1, 0)).astype(BF16)


def pick_kernel(plan, a_ref, b_ref, own_ref, send_ref):
    y, m = where_am_i(plan)
    blk = plan.block
    mine = pl.ds(pl.multiple_of(y * blk, blk), blk)
    theirs = pl.ds(pl.multiple_of((plan.g - 1 - y) * blk, blk), blk)
    for i, ref in enumerate((a_ref, b_ref)):
        own_ref[i * blk : (i + 1) * blk, :] = ref[mine, :]
        send_ref[i * blk : (i + 1) * blk, :] = ref[theirs, :]


def join_kernel(plan, own_ref, got_ref, a_ref, b_ref):
    y, m = where_am_i(plan)
    blk = plan.block
    left = pl.ds(pl.multiple_of(y * plan.w, plan.w), plan.w)
    right = pl.ds(pl.multiple_of((plan.g - 1 - y) * plan.w, plan.w), plan.w)
    for i, ref in enumerate((a_ref, b_ref)):
        ref[:, left] = own_ref[i * blk : (i + 1) * blk, :]
        if plan.g > 1:
            ref[:, right] = got_ref[i * blk : (i + 1) * blk, :]


def spread(plan, f):
    return f[: plan.hl, 0][:, None, None]


def tiles(plan, t):
    return t.reshape(plan.hl, DK, DK)


def flat(plan, t):
    return t.reshape(plan.hl * DK, DK)


def forward_scan(plan, total, total_b, f):
    z = lax.axis_index("seq") // plan.g
    total = tiles(plan, total)
    if not power_of_two(plan.nz):
        acc, facc, by, kept = total, f, 1, []
        while by < plan.nz:
            pairs = plan.shift_pairs(by)
            got = lax.ppermute(acc.astype(BF16), AXES, pairs).astype(F32)
            fgot = lax.ppermute(facc, AXES, pairs)
            acc = spread(plan, facc) * got + acc
            facc = facc * fgot
            by *= 2
        return flat(plan, lax.ppermute(acc.astype(BF16), AXES, plan.shift_pairs(1)).astype(F32)), f
    state = jnp.zeros_like(total)
    before = jnp.ones_like(f)
    after = jnp.ones_like(f)
    ftotal, flip, kept = f, 1, []
    while flip < plan.nz:
        pairs = plan.scan_pairs(flip)
        late = (z & flip) != 0
        got = tiles(plan, lax.ppermute(total_b, AXES, pairs)).astype(F32)
        state = jnp.where(late, spread(plan, before) * got + state, state)
        if flip * 2 < plan.nz:
            fgot = lax.ppermute(ftotal, AXES, pairs)
            kept.append((flip, late, ftotal, fgot, after))
            total = jnp.where(
                late, spread(plan, ftotal) * got + total, spread(plan, fgot) * total + got
            )
            total_b = flat(plan, total.astype(BF16))
            before = jnp.where(late, before * fgot, before)
            after = jnp.where(late, after, after * fgot)
            ftotal = ftotal * fgot
        else:
            kept.append((flip, late, ftotal, None, after))
        flip *= 2
    return flat(plan, state), kept


def backward_scan(plan, total, total_b, kept):
    total = tiles(plan, total)
    if not power_of_two(plan.nz):
        acc, facc, by = total, kept, 1
        while by < plan.nz:
            pairs = plan.shift_pairs(-by)
            got = lax.ppermute(acc.astype(BF16), AXES, pairs).astype(F32)
            fgot = lax.ppermute(facc, AXES, pairs)
            acc = spread(plan, facc) * got + acc
            facc = facc * fgot
            by *= 2
        return flat(plan, lax.ppermute(acc.astype(BF16), AXES, plan.shift_pairs(-1)).astype(F32))
    state = jnp.zeros_like(total)
    for flip, late, ftotal, fgot, after in kept:
        got = tiles(plan, lax.ppermute(total_b, AXES, plan.scan_pairs(flip))).astype(F32)
        state = jnp.where(late, state, spread(plan, after) * got + state)
        if fgot is not None:
            total = jnp.where(
                late, spread(plan, fgot) * total + got, spread(plan, ftotal) * got + total
            )
            total_b = flat(plan, total.astype(BF16))
    return flat(plan, state)


def local(queries, keys, values, log_decay, out_grad):
    plan = Plan(
        lax.axis_size("seq"),
        lax.axis_size("head"),
        queries.shape[0],
        log_decay.shape[0],
        log_decay.shape[1],
    )
    n, tok, w, tb, hl, blk = plan.n, plan.tok, plan.w, plan.tb, plan.hl, plan.block
    part = functools.partial
    *sends, ld_own = call(
        part(pack_kernel, plan),
        [struct((3 * tok, w), BF16)] * n + [struct((plan.heads, blk), F32)],
        (queries, keys, values, log_decay),
        "pack",
    )
    parts = [sends[0]] + [
        lax.ppermute(sends[p], AXES, plan.member_pairs(p)) for p in range(1, n)
    ]
    if plan.g > 1:
        ld_other = lax.ppermute(ld_own, AXES, plan.mate_pairs())
        grad_own, grad_send = call(
            part(split_kernel, plan), [struct((blk, w), BF16)] * 2, (out_grad,), "split"
        )
        grad_other = lax.ppermute(grad_send, AXES, plan.mate_pairs())
    else:
        ld_other, grad_own, grad_other = ld_own, out_grad, out_grad
    wide = struct((tb, w), BF16)
    wide32 = struct((tb, w), F32)
    square = struct((w, DK), F32)
    squareb = struct((w, DK), BF16)
    q, k, v, row, col, own_state, own_state_b, f = call(
        part(state_kernel, plan),
        [
            wide,
            wide,
            wide,
            struct((plan.rows, tb), F32),
            struct((tb, 128), F32),
            square,
            squareb,
            struct((plan.rows, 128), F32),
        ],
        (*parts, ld_own, ld_other),
        "state",
    )
    one = 2 * hl * tb * tb * DK
    state_in, kept = forward_scan(plan, own_state, own_state_b, f)
    weighted, inner = call(
        part(inner_kernel, plan),
        [struct((hl, tb, tb), BF16), wide32],
        (q, k, v, row, col),
        "inner",
        2 * one,
    )
    out, od, own_grad, own_grad_b = call(
        part(mix_kernel, plan),
        [wide, wide, square, squareb],
        (q, inner, state_in, grad_own, grad_other, col),
        "mix",
        one,
        scratch=[pltpu.VMEM((tb, w), BF16)],
    )
    grad_in = backward_scan(plan, own_grad, own_grad_b, kept)
    qg, kp, vp = call(
        part(back_kernel, plan),
        [wide, wide32, wide32],
        (q, k, v, row, col, weighted, od, state_in),
        "back",
        5 * one,
    )
    kg, vg = call(
        part(last_kernel, plan), [wide, wide], (k, v, col, kp, vp, grad_in), "last", one
    )
    if plan.g == 1:
        return out, qg, kg, vg
    results = []
    pair = struct((2 * blk, w), BF16)
    final = struct((blk, 2 * w), BF16)
    for a, b, tag in ((out, qg, "first"), (kg, vg, "second")):
        own, send = call(part(pick_kernel, plan), [pair, pair], (a, b), "pick_" + tag)
        got = lax.ppermute(send, AXES, plan.mate_pairs())
        results += call(part(join_kernel, plan), [final, final], (own, got), "join_" + tag)
    return tuple(results)


def solution(mesh):
    placed = (
        P(("seq", "head"), None),
        P(("seq", "head"), None),
        P(("seq", "head"), None),
        P("seq", "head"),
        P("seq", "head"),
    )
    return jax.shard_map(
        local,
        mesh=mesh,
        in_specs=placed,
        out_specs=(P("seq", "head"), P("seq", "head"), P("seq", "head"), P("seq", "head")),
        check_vma=False,
    )
```
